128 devices in a mesh: seq: 2 (over core), ctx: 16 (over y, x), tp: 4 (over z).
Axes of the slice: x: 4, y: 4, z: 4, core: 2. Of those that a mesh axis runs over, the one named last changes fastest.
Arguments:
- queries: bfloat16 [24576, 4096], P(('seq', 'ctx'), 'tp'), parts along dimension 0, may hold values from -6 to 6
- key_rows: bfloat16 [24576, 4096], P(('seq', 'ctx'), 'tp'), parts along dimension 0, may hold values from -6 to 6
- value_rows: bfloat16 [24576, 4096], P(('seq', 'ctx'), 'tp'), parts along dimension 0, may hold values from -60 to 60, as said below
- doc_ids: int32 [24576], P(('seq', 'ctx')), parts along dimension 0, may hold values from 0 to 31, never falling along the last dimension, each value on 1 to 6144 neighbouring positions
- norm_gain: float32 [4096], P('tp'), may hold values from 0.5 to 1.5
- out_weight: bfloat16 [4096, 4096], P('tp', 'ctx'), may hold values from -0.125 to 0.125
- out_grad: bfloat16 [24576, 4096], P(('seq', 'ctx'), 'tp'), parts along dimension 0, may hold values from -6 to 6
Outputs:
- layer_out: bfloat16 [24576, 4096], P(('seq', 'ctx'), 'tp'), parts along dimension 0
- query_grad: bfloat16 [24576, 4096], P(('seq', 'ctx'), 'tp'), parts along dimension 0
- key_grad: bfloat16 [24576, 4096], P(('seq', 'ctx'), 'tp'), parts along dimension 0
- value_grad: bfloat16 [24576, 4096], P(('seq', 'ctx'), 'tp'), parts along dimension 0
- weight_grad: bfloat16 [8192, 4096], P(('seq', 'tp'), 'ctx'), parts along dimension 0
- gain_grad: float32 [8192], P(('seq', 'tp')), parts along dimension 0
The draws below stay inside these ranges and needn't reach their ends.
There are 2 independent parts, one for each index of `seq`. The reference program is written for one: setup_inputs(seed, part) draws one part's arguments, and reference() takes and returns one part's arrays. A program takes and returns all parts, laid end to end along the dimension named above; an argument that names none is the same for every part. Nothing has to cross between parts.
Inputs may be any that keep to these rules, and one draw needn't show every extreme that they name: `doc_ids`: document numbers never fall along the sequence; every number occurs; a document takes 1 to 6144 positions and one takes exactly that many. `value_rows`: real values, columns of differing scale.
All inputs are finite; a program needn't handle non-finite values.
Results may differ from the reference program's by a relative error of at most 0.019.
Values may be sent and summed in bfloat16 or wider, within the bound.
No kernel may reach another device: no remote copies, remote signals or barrier semaphores. Data moves between devices by JAX's collectives and lax.ppermute only.
A program may use at most 128 MiB of HBM per device.

```python
import math
import jax
import jax.numpy as jnp
import numpy as np
from jax import lax

HEADS = 32
HEAD_DIM = 128
D = 4096
TOK_DEV = 768
PANEL = 256
BLOCK = 16
LENGTH = 12288
DOCS = 32
N_CTX = 16
N_TP = 4


def draw_value_rows(key, part):
    base_key, scale_key = jax.random.split(jax.random.fold_in(key, 7), 2)
    columns = jnp.exp(jax.random.uniform(scale_key, (1, D), jnp.float32, 0.0, math.log(10.0)))
    values = columns * jax.random.normal(base_key, (LENGTH, D), jnp.float32)
    return jnp.clip(values, -60.0, 60.0).astype(jnp.bfloat16)


def spiked(entries, rng, source, target, shards_of, factor):
    def block_of(position):
        return (jnp.arange(entries.shape[position]) // (entries.shape[position] // shards_of)).reshape((-1,) + (1,) * (entries.ndim - 1 - position))

    first = jax.random.permutation(rng, shards_of)[block_of(target)]
    far = (block_of(target) + shards_of // 2) % shards_of
    return jnp.where((block_of(source) == first) | (block_of(source) == far), factor * entries, entries)


def shard_levels(rng, shape, cuts, low, top_value):
    def one(position, shards_of):
        heights = jax.random.uniform(jax.random.fold_in(jax.random.fold_in(rng, 6), position), (shards_of,), jnp.float32, low / len(cuts), top_value / len(cuts))
        return jnp.repeat(jnp.exp(heights), shape[position] // shards_of).reshape((-1,) + (1,) * (len(shape) - position - 1))

    factor_of = one(*cuts[0])
    for cut in cuts[1:]:
        factor_of = factor_of * one(*cut)
    return factor_of


def length_profile(count, total, bound, slope):
    weights = [(1 << 20) // math.isqrt(rank ** slope) + 1 for rank in range(2, count + 1)]
    spare, holding = total - bound - (count - 1), [1] * (count - 1)
    while spare > 0:
        free = [i for i in range(count - 1) if holding[i] < bound]
        mass, remaining = sum([weights[i] for i in free]), spare
        for i in free:
            extra = min(bound - holding[i], max(1, remaining * weights[i] // mass), spare)
            holding[i] = holding[i] + extra
            spare = spare - extra
    return np.array([bound] + holding)


def ragged_sizes(rng, count, total, limit, skew):
    if count == 2:
        one = jax.random.randint(rng, (), max(1, total - limit), min(limit, total - 1) + 1)
        return jnp.stack([one, total - one])
    tallies = jnp.asarray(length_profile(count, total, limit, skew), jnp.int32)
    twos = (count - 1) // 2
    donor, sink = tallies[1:1 + 2 * twos:2], tallies[2:2 + 2 * twos:2]
    margin = jnp.minimum(donor - 1, limit - sink)
    moved = jax.random.randint(jax.random.fold_in(rng, 1), (twos,), 0, 1 << 20) % (margin + 1)
    tallies = tallies.at[1:1 + 2 * twos:2].set(donor - moved).at[2:2 + 2 * twos:2].set(sink + moved)
    return tallies[jax.random.permutation(jax.random.fold_in(rng, 2), count)]


def normal_values(rng, dims, scale, most, cuts=(), kind=jnp.bfloat16):
    entries = jax.random.normal(rng, dims, jnp.float32) * scale
    if len(cuts) > 0:
        entries = shard_levels(rng, dims, cuts, -0.22, 0.18) * entries
    return jnp.clip(entries, min=-most, max=most).astype(kind)


def noise_with(key, extent, scale, reach, shards, heavy, kind=jnp.bfloat16):
    drawn = scale * jax.random.normal(key, extent, jnp.float32)
    if shards:
        drawn = drawn * shard_levels(key, extent, shards, -0.22, 0.18)
    return jnp.clip(spiked(drawn, jax.random.fold_in(key, 3), *heavy), -reach, reach).astype(kind)


def setup_inputs(seed: int = 0, part: int = 0) -> dict:
    splits = jax.random.split(jax.random.key(seed), 8)
    part_keys = jax.random.split(jax.random.fold_in(splits[7], part), 8)
    return {
        "queries": normal_values(part_keys[0], (LENGTH, D), 1.0, 6.0, ((0, 16), (1, 4))),
        "key_rows": normal_values(part_keys[1], (LENGTH, D), 1.0, 6.0, ((0, 16), (1, 4))),
        "value_rows": draw_value_rows(jax.random.fold_in(jax.random.fold_in(splits[7], part), 71), part),
        "doc_ids": jnp.searchsorted(jnp.cumsum(ragged_sizes(part_keys[3], DOCS, LENGTH, LENGTH // 2, 2)), jnp.arange(LENGTH), side="right").astype(jnp.int32),
        "norm_gain": jnp.clip(1.0 + 0.1 * jax.random.normal(splits[4], (D,), jnp.float32), 0.5, 1.5),
        "out_weight": noise_with(splits[5], (D, D), D ** -0.5, 0.125, ((0, 4), (1, 16)), (0, 1, 16, 2.0)),
        "out_grad": noise_with(part_keys[6], (LENGTH, D), 1.0, 6.0, ((0, 16), (1, 4)), (0, 1, 16, 2.0)),
    }


EPS = 1e-05
FAR = 2 ** 30
HIGHEST = lax.Precision.HIGHEST

def einsum_full(form, left, right):
    return jnp.einsum(form, left, right, precision=HIGHEST)

def rounded(value):
    return lax.optimization_barrier(value.astype(jnp.bfloat16)).astype(jnp.float32)

def panel_mask(docs):
    blocks = jnp.arange(docs.shape[0], dtype=jnp.int32) // BLOCK
    same = docs[:, None] == docs[None, :]
    seen = blocks[None, :] <= blocks[:, None]
    return (same & seen).astype(jnp.float32)

def forward_panel(carry, inputs):
    state, last = carry
    query, key, value, docs = inputs
    allowed = panel_mask(docs)
    scores = rounded(einsum_full('thd,shd->hts', query, key) * allowed[None])
    inner = einsum_full('hts,shd->thd', scores, value)
    state_low = rounded(state)
    usage = (docs == last).astype(jnp.float32)
    cross = einsum_full('thd,hde->the', query, state_low) * usage[:, None, None]
    ending = docs[-1]
    keeper = (docs == ending).astype(jnp.float32)
    summary = einsum_full('thd,the->hde', key * keeper[:, None, None], value)
    state_next = jnp.where(ending > last, summary, state + summary)
    return ((state_next, ending), (inner + cross, state_low, usage))

def backward_panel(carry, inputs):
    later, first = carry
    query, key, value, docs, upstream, state_low, usage = inputs
    allowed = panel_mask(docs)
    scores = rounded(einsum_full('thd,shd->hts', query, key) * allowed[None])
    score_grad = rounded(einsum_full('the,she->hts', upstream, value) * allowed[None])
    later_low = rounded(later)
    later_use = (docs == first).astype(jnp.float32)[:, None, None]
    query_grad = einsum_full('hts,shd->thd', score_grad, key) + usage[:, None, None] * einsum_full('the,hde->thd', upstream, state_low)
    key_grad = einsum_full('hts,thd->shd', score_grad, query) + later_use * einsum_full('she,hde->shd', value, later_low)
    value_grad = einsum_full('hts,the->she', scores, upstream) + later_use * einsum_full('shd,hde->she', key, later_low)
    opening = docs[0]
    keeper = (docs == opening).astype(jnp.float32)
    summary = einsum_full('thd,the->hde', query * keeper[:, None, None], upstream)
    later_next = jnp.where(opening < first, summary, later + summary)
    return ((later_next, opening), (query_grad, key_grad, value_grad))

def reference(queries, key_rows, value_rows, doc_ids, norm_gain, out_weight, out_grad):
    panels = LENGTH // PANEL

    def heads_of(rows):
        return rows.astype(jnp.float32).reshape(panels, PANEL, HEADS, HEAD_DIM)
    query, key, value = (heads_of(queries), heads_of(key_rows), heads_of(value_rows))
    docs = doc_ids.reshape(panels, PANEL)
    zero_state = jnp.zeros((HEADS, HEAD_DIM, HEAD_DIM), jnp.float32)
    _, (raw, state_low, usage) = lax.scan(forward_panel, (zero_state, jnp.array(-1, jnp.int32)), (query, key, value, docs))
    raw = raw.reshape(LENGTH, HEADS, HEAD_DIM)
    scale = lax.rsqrt(lax.optimization_barrier(jnp.mean(raw * raw, axis=-1, keepdims=True)) + EPS)
    normed = raw * scale
    gain = norm_gain.reshape(HEADS, HEAD_DIM)
    mixed = (normed * gain).astype(jnp.bfloat16).reshape(LENGTH, D)
    group = D // N_TP
    total = jnp.zeros((LENGTH, D), jnp.float32)
    for index in range(N_TP):
        total = total + rounded(jnp.dot(mixed[:, index * group:(index + 1) * group], out_weight[index * group:(index + 1) * group], preferred_element_type=jnp.float32))
    layer_out = total.astype(jnp.bfloat16)
    upward = jnp.dot(out_grad, out_weight.T, preferred_element_type=jnp.float32).reshape(LENGTH, HEADS, HEAD_DIM)
    weight_total = jnp.zeros((D, D), jnp.float32)
    for index in range(N_CTX):
        weight_total = weight_total + rounded(jnp.dot(mixed[index * TOK_DEV:(index + 1) * TOK_DEV].T, out_grad[index * TOK_DEV:(index + 1) * TOK_DEV], preferred_element_type=jnp.float32))
    weight_grad = weight_total.astype(jnp.bfloat16)
    gain_grad = lax.optimization_barrier(jnp.sum(upward * normed, axis=0)).reshape(D)
    scaled = upward * gain
    centre = lax.optimization_barrier(jnp.mean(scaled * normed, axis=-1, keepdims=True))
    upstream = rounded(scale * (scaled - normed * centre)).reshape(panels, PANEL, HEADS, HEAD_DIM)
    _, (query_grad, key_grad, value_grad) = lax.scan(backward_panel, (zero_state, jnp.array(FAR, jnp.int32)), (query, key, value, docs, upstream, state_low, usage), reverse=True)
    return (layer_out, query_grad.reshape(LENGTH, D).astype(jnp.bfloat16), key_grad.reshape(LENGTH, D).astype(jnp.bfloat16), value_grad.reshape(LENGTH, D).astype(jnp.bfloat16), weight_grad, gain_grad)
```

```python
import functools

import jax
import jax.numpy as jnp
from jax import lax
from jax.experimental import pallas as pl
from jax.experimental.pallas import tpu as pltpu
from jax.sharding import PartitionSpec as P

HD = 128
PANEL = 256
BLOCK = 16
EPS = 1e-05
F32 = jnp.float32
BF16 = jnp.bfloat16


def dot(a, b, ca=1, cb=0):
    return lax.dot_general(a, b, (((ca,), (cb,)), ((), ())), preferred_element_type=F32)


def along_tp(step):
    return [(i, (i + step) % 4) for i in range(4)]


def along_grid(axis_of_seq, step):
    pairs = []
    for s in range(2):
        for y in range(4):
            for x in range(4):
                if axis_of_seq[s] == "y":
                    to = ((y + step) % 4) * 4 + x
                else:
                    to = y * 4 + (x + step) % 4
                pairs.append((s * 16 + y * 4 + x, s * 16 + to))
    return pairs


YX = ("y", "x")
XY = ("x", "y")


def grid_perm(value, axis_of_seq, step):
    return lax.ppermute(value, ("seq", "ctx"), along_grid(axis_of_seq, step))


def tp_perm(value, step):
    return lax.ppermute(value, "tp", along_tp(step))


def ring_gather(own, send):
    half = own.shape[-2] // 2
    prev = send(own, 1)
    succ = send(own, -1)
    far_low = send(prev[..., :half, :], 1)
    far_high = send(succ[..., half:, :], -1)
    return prev, succ, far_low, far_high


def total(*parts):
    out = parts[0].astype(F32)
    for part in parts[1:]:
        out = out + part.astype(F32)
    return out.astype(BF16)


def ring_scatter(far, rest, send):
    low, high = send(far[0], 1), send(far[1], -1)
    succ, prev, own = rest()
    half = succ.shape[0] // 2
    up = jnp.concatenate([total(succ[:half], low), succ[half:]])
    down = jnp.concatenate([prev[:half], total(prev[half:], high)])
    return total(own, send(up, 1), send(down, -1))


def direct_scatter(far, succ, prev, own, send):
    return total(own, send(far, 2), send(succ, 1), send(prev, -1))


def around(value, step):
    return lax.ppermute(value, "ctx", [(i, (i + step) % 16) for i in range(16)])


def join(near, far, near_ok, far_ok):
    slot = lax.broadcasted_iota(jnp.int32, near.shape, 0)
    row = lax.broadcasted_iota(jnp.int32, near.shape, 1)
    gains = (slot == 8) & (row >= 16)
    same = ((far[8, 0, 0] == near[8, 0, 0]) & far_ok).astype(F32)
    keep = jnp.where(gains, 1.0, near_ok.astype(F32))
    add = jnp.where(gains, 1.0, jnp.where(slot < 8, same, 0.0))
    return (near.astype(F32) * keep + far.astype(F32) * add).astype(BF16)


def window(own, sign, c):
    back = c if sign > 0 else 15 - c
    first = around(own, sign)
    second = around(own, 2 * sign)
    true = jnp.bool_(True)
    held = join(first, second, back >= 1, back >= 2)
    held = join(held, around(held, 2 * sign), true, back >= 2)
    return join(held, around(held, 4 * sign), true, back >= 4)


def whole(shape):
    return pl.BlockSpec(shape, lambda *_: (0,) * len(shape))


def call(kernel, grid, in_specs, out_specs, out_shape, scratch=(), prefetch=0, name=None):
    return pl.pallas_call(
        kernel,
        grid_spec=pltpu.PrefetchScalarGridSpec(
            num_scalar_prefetch=prefetch,
            grid=grid,
            in_specs=in_specs,
            out_specs=out_specs,
            scratch_shapes=scratch,
        ),
        out_shape=out_shape,
        name=name,
        compiler_params=pltpu.CompilerParams(vmem_limit_bytes=56 * 1024 * 1024),
    )


def sums_kernel(k_ref, v_ref, dcol_ref, out_ref):
    j = pl.program_id(0)
    docs = dcol_ref[...]
    end = docs[-1:, :]
    keep = (docs == end).astype(BF16)
    for h in range(2):
        cols = slice(h * HD, (h + 1) * HD)
        out_ref[2 * j + h] = dot(k_ref[:, cols] * keep, v_ref[:, cols], 0, 0).astype(BF16)

    @pl.when(j == 0)
    def _():
        out_ref[8] = jnp.zeros((HD, HD), BF16)
        out_ref[8, :16] = jnp.broadcast_to(end, (16, HD)).astype(BF16)


def fill_masks(mask_ref, dcol_ref, drow_ref):
    for p in range(3):
        rows = slice(p * PANEL, (p + 1) * PANEL)
        t = lax.broadcasted_iota(jnp.int32, (PANEL, PANEL), 0) // BLOCK
        s = lax.broadcasted_iota(jnp.int32, (PANEL, PANEL), 1) // BLOCK
        same = dcol_ref[rows, :1] == drow_ref[:1, rows]
        mask_ref[p] = (same & (s <= t)).astype(F32)


def forward_kernel(
    q_ref, k_ref, v_ref, dcol_ref, drow_ref, gain_ref, carry_ref, slot_ref,
    mixed_ref, mixed_t_ref, raw_ref, low_ref, mask_ref,
):
    @pl.when(pl.program_id(0) == 0)
    def _():
        fill_masks(mask_ref, dcol_ref, drow_ref)

    for h in range(2):
        cols = slice(h * HD, (h + 1) * HD)
        state = carry_ref[h].astype(F32)
        doc = slot_ref[0, :1, :].astype(F32)
        gain = gain_ref[:, cols]
        for p in range(3):
            rows = slice(p * PANEL, (p + 1) * PANEL)
            q, k, v, docs = q_ref[rows, cols], k_ref[rows, cols], v_ref[rows, cols], dcol_ref[rows]
            scores = (dot(q, k, 1, 1) * mask_ref[p]).astype(BF16)
            low = state.astype(BF16)
            low_ref[h, p] = low
            raw = dot(scores, v) + (docs == doc).astype(F32) * dot(q, low)
            raw_ref[rows, cols] = raw
            scale = lax.rsqrt(jnp.mean(raw * raw, axis=-1, keepdims=True) + EPS)
            mixed = (raw * scale * gain).astype(BF16)
            mixed_ref[rows, cols] = mixed
            mixed_t_ref[cols, rows] = mixed.T
            if p < 2:
                end = docs[-1:, :]
                summary = dot(k * (docs == end).astype(BF16), v, 0, 0)
                state = jnp.where(end == doc, state, 0.0) + summary
                doc = end


G_PARTS = ((0, 0, 768), (3, 0, 768), (1, 0, 768), (2, 0, 384), (2, 384, 384))
W_PARTS = ((0, 0, 512), (3, 0, 512), (1, 0, 512), (2, 0, 256), (2, 256, 256))


def start_grad(w_ref, parts, g_ref, sem):
    for part, (off, row, rows) in zip(parts, G_PARTS):
        at = lax.rem(w_ref[3] + off, 4)
        pltpu.make_async_copy(part, g_ref.at[at, pl.ds(row, rows)], sem.at[at]).start()


def start_weight(w_ref, parts, full_ref, sem, half, wanted=None):
    s = w_ref[0]
    for mine in (True, False):
        base, inner = (w_ref[5], w_ref[4]) if mine else (w_ref[4], w_ref[5])

        def copies(mine=mine, base=base, inner=inner):
            for n, (off, row, rows) in enumerate(W_PARTS):

                @pl.loop(0, 4)
                def _(m, n=n, off=off, row=row, rows=rows):
                    a, b = lax.rem(base + off, 4), lax.rem(inner + m, 4)
                    copy = pltpu.make_async_copy(
                        parts[n + (0 if mine else 5)].at[m],
                        full_ref.at[half, a, b, pl.ds(row, rows)],
                        sem.at[half, a, b],
                    )
                    if wanted is None:
                        copy.start()
                    else:
                        pl.when(wanted(a, b))(copy.start)

        pl.when((s == half) if mine else (s != half))(copies)


def wait_for(ref, sem):
    pltpu.make_async_copy(ref, ref, sem).wait()


def upward_kernel(w_ref, *refs):
    parts, refs = refs[:15], refs[15:]
    raw_ref, q_ref, gain_ref, dcol_ref, up_ref, later_ref, acc_ref, part_ref, g_ref, full_ref, g_sem, w_sem = refs
    j = pl.program_id(0)

    @pl.when(j == 0)
    def _():
        start_grad(w_ref, parts[:5], g_ref, g_sem)
        start_weight(w_ref, parts[5:], full_ref, w_sem, 0)
        start_weight(w_ref, parts[5:], full_ref, w_sem, 1)
        part_ref[...] = jnp.zeros_like(part_ref)
        for y in range(4):
            wait_for(g_ref.at[y], g_sem.at[y])

    rows = pl.ds(pl.multiple_of(lax.rem(j, 2) * 256, 256), 256)
    for half in range(2):

        @pl.when(j == 2 * half)
        def _(half=half):
            for y in range(4):
                for x in range(4):
                    wait_for(full_ref.at[half, y, x], w_sem.at[half, y, x])

        @pl.when(j // 2 == half)
        def _(half=half):
            acc = None
            for y in range(4):
                at = lambda x: (half, y, x, rows) if half == 0 else (half, x, y, rows)
                blocks = [full_ref[at(x)] for x in range(4)]
                new = dot(g_ref[y], jnp.concatenate(blocks, axis=1), 1, 1)
                acc = new if y == 0 else acc + new
            acc_ref[...] = acc

    docs = dcol_ref[...]
    start = docs[:1, :]
    keep = (docs == start).astype(BF16)
    for h in range(2):
        cols = slice(h * HD, (h + 1) * HD)
        up = acc_ref[:, cols]
        raw = raw_ref[:, cols]
        scale = lax.rsqrt(jnp.mean(raw * raw, axis=-1, keepdims=True) + EPS)
        normed = raw * scale
        part = jnp.sum(up * normed, axis=0, keepdims=True)
        part_ref[pl.ds(2 * j + h, 1), :] = part
        scaled = up * gain_ref[:, cols]
        centre = jnp.mean(scaled * normed, axis=-1, keepdims=True)
        stream = (scale * (scaled - normed * centre)).astype(BF16)
        up_ref[:, cols] = stream
        later_ref[2 * j + h] = dot(q_ref[:, cols] * keep, stream, 0, 0).astype(BF16)

    @pl.when(j == 3)
    def _():
        later_ref[8] = jnp.zeros((HD, HD), BF16)
        later_ref[8, :16] = jnp.broadcast_to(start, (16, HD)).astype(BF16)
        later_ref[8, 16:32] = part_ref[...].astype(BF16)


def project_kernel(steps, w_ref, *refs):
    parts, mixed_ref, refs = refs[:10], refs[10], refs[11:]
    outs, (full_ref, sem) = refs[:-2], refs[-2:]
    z = w_ref[3]
    if steps == (2,):
        far = lax.rem(z + 2, 4)
        start_weight(w_ref, parts, full_ref, sem, 0, lambda a, b: a == far)
        start_weight(w_ref, parts, full_ref, sem, 1, lambda a, b: b == far)
    else:
        far = lax.rem(z + 2, 4)
        start_weight(w_ref, parts, full_ref, sem, 0, lambda a, b: a != far)
        start_weight(w_ref, parts, full_ref, sem, 1, lambda a, b: b != far)
    for n, r in enumerate(steps):
        to = lax.rem(z + r, 4)
        for i in range(4):
            wait_for(full_ref.at[0, to, i], sem.at[0, to, i])
            wait_for(full_ref.at[1, i, to], sem.at[1, i, to])
        for i in range(4):
            cols = slice(i * 256, (i + 1) * 256)
            w = jnp.concatenate([full_ref[0, to, i], full_ref[1, i, to]], axis=0)
            out = dot(mixed_ref[...], w).astype(BF16)
            if r == 2:
                outs[0][:, cols] = out[:384]
                outs[1][:, cols] = out[384:]
            else:
                outs[n][:, cols] = out


def weight_kernel(steps, w_ref, *refs):
    parts, mixed_t_ref, refs = refs[:5], refs[5], refs[6:]
    outs, (g_ref, sem) = refs[:-2], refs[-2:]
    zero = w_ref[0] == 0
    for n, r in enumerate(steps):

        @pl.loop(0, 4)
        def _(i, n=n, r=r):
            row = jnp.where(zero, lax.rem(w_ref[1] + r, 4), i)
            col = jnp.where(zero, i, lax.rem(w_ref[2] + r, 4))
            cols = pl.ds(pl.multiple_of(col * 256, 256), 256)
            for part, (off, at, rows) in zip(parts, G_PARTS):
                copy = pltpu.make_async_copy(
                    part.at[:, cols], g_ref.at[n, i, pl.ds(at, rows)], sem.at[n, i]
                )
                pl.when(lax.rem(w_ref[3] + off, 4) == row)(copy.start)
    for n, r in enumerate(steps):
        for i in range(4):
            wait_for(g_ref.at[n, i], sem.at[n, i])
        for i in range(4):
            out = dot(mixed_t_ref[...], g_ref[n, i]).astype(BF16)
            if r == 2:
                outs[i // 2][i % 2] = out
            else:
                outs[n][i] = out


def backward_kernel(
    q_ref, k_ref, v_ref, u_ref, dcol_ref, drow_ref, low_ref, prev_ref, later_ref, slot_ref,
    qg_ref, kg_ref, vg_ref, mask_ref,
):
    @pl.when(pl.program_id(0) == 0)
    def _():
        fill_masks(mask_ref, dcol_ref, drow_ref)

    for h in range(2):
        cols = slice(h * HD, (h + 1) * HD)
        later = later_ref[h].astype(F32)
        doc = slot_ref[0, :1, :].astype(F32)
        for p in (2, 1, 0):
            rows = slice(p * PANEL, (p + 1) * PANEL)
            q, k, v, u = q_ref[rows, cols], k_ref[rows, cols], v_ref[rows, cols], u_ref[rows, cols]
            docs = dcol_ref[rows]
            before = prev_ref[0, :1, :].astype(F32) if p == 0 else dcol_ref[p * PANEL - 1 : p * PANEL, :]
            mask = mask_ref[p]
            scores = (dot(q, k, 1, 1) * mask).astype(BF16)
            grads = (dot(u, v, 1, 1) * mask).astype(BF16)
            later_low = later.astype(BF16)
            usage = (docs == before).astype(F32)
            use = (docs == doc).astype(F32)
            qg_ref[rows, cols] = (dot(grads, k) + usage * dot(u, low_ref[h, p], 1, 1)).astype(BF16)
            kg_ref[rows, cols] = (dot(grads, q, 0, 0) + use * dot(v, later_low, 1, 1)).astype(BF16)
            vg_ref[rows, cols] = (dot(scores, u, 0, 0) + use * dot(k, later_low)).astype(BF16)
            if p > 0:
                start = docs[:1, :]
                summary = dot(q * (docs == start).astype(BF16), u, 0, 0)
                later = jnp.where(start == doc, later, 0.0) + summary
                doc = start


def local(q, k, v, doc_ids, norm_gain, weight, grad):
    s, c, z = lax.axis_index("seq"), lax.axis_index("ctx"), lax.axis_index("tp")
    y, x = c // 4, c % 4
    gain = norm_gain.reshape(1, 1024)
    docs = (doc_ids + 1).astype(F32)
    dcol = jnp.broadcast_to(docs[:, None], (768, HD))
    drow = docs.reshape(1, 768)
    sds = jax.ShapeDtypeStruct

    pair = pl.BlockSpec((768, 256), lambda j, *_: (0, j))

    g_prev, g_succ, g_low, g_high = ring_gather(grad, tp_perm)

    sums = call(
        sums_kernel, (4,), [pair] * 2 + [whole((768, HD))], whole((9, HD, HD)),
        sds((9, HD, HD), BF16), name="sums",
    )(k, v, dcol)
    carry = window(sums, 1, c)

    first = jnp.where(s == 0, x, y)
    second = jnp.where(s == 0, y, x)
    where = jnp.stack([s, y, x, z, first, second]).astype(jnp.int32)
    mine = lax.dynamic_slice_in_dim(weight, s * 512, 512, 0)
    send1 = lambda value, step: grid_perm(value, XY, step)
    send2 = lambda value, step: grid_perm(value, YX, step)
    line = jnp.stack([mine, send1(mine, -1), send1(mine, 2), send1(mine, 1)])
    lines = (line,) + ring_gather(line, send2)
    swapped = tuple(lax.ppermute(piece, "seq", [(0, 1), (1, 0)]) for piece in lines)
    weights = lines + swapped

    slot = pl.BlockSpec((1, HD, HD), lambda h, *_: (8, 0, 0))
    per = pl.BlockSpec((2, HD, HD), lambda h, *_: (h, 0, 0))
    lows = pl.BlockSpec((2, 3, HD, HD), lambda h, *_: (h, 0, 0, 0))
    masks = [pltpu.VMEM((3, PANEL, PANEL), F32)]
    mixed, mixed_t, raw, low = call(
        forward_kernel, (4,),
        [pair] * 3 + [whole((768, HD)), whole((1, 768)), pl.BlockSpec((1, 256), lambda h: (0, h)), per, slot],
        [pair, pl.BlockSpec((256, 768), lambda h: (h, 0)), pair, lows],
        [sds((768, 1024), BF16), sds((1024, 768), BF16), sds((768, 1024), F32), sds((8, 3, HD, HD), BF16)],
        masks, name="forward",
    )(q, k, v, dcol, drow, gain, carry, carry)

    anywhere = pl.BlockSpec(memory_space=pl.ANY)
    w_scratch = [pltpu.VMEM((2, 4, 4, 512, 256), BF16), pltpu.SemaphoreType.DMA((2, 4, 4))]
    g_scratch = [pltpu.VMEM((4, 768, 1024), BF16), pltpu.SemaphoreType.DMA((4,))]

    def project(*steps):
        shapes = [(384, 1024)] * 2 if steps == (2,) else [(768, 1024)] * len(steps)
        return call(
            functools.partial(project_kernel, steps), (1,),
            [anywhere] * 10 + [whole((768, 1024))], [whole(h) for h in shapes],
            [sds(h, BF16) for h in shapes], w_scratch, prefetch=1, name=f"project{steps[0]}",
        )(where, *weights, mixed)

    layer_out = ring_scatter(project(2), lambda: project(1, 3, 0), tp_perm)

    grads = (grad, g_prev, g_succ, g_low, g_high)
    up, later_sums = call(
        upward_kernel, (4,),
        [anywhere] * 15 + [pair, pair, pl.BlockSpec((1, 256), lambda j, *_: (0, j)), whole((768, HD))],
        [pair, whole((9, HD, HD))],
        [sds((768, 1024), BF16), sds((9, HD, HD), BF16)],
        [pltpu.VMEM((768, 256), F32), pltpu.VMEM((16, HD), F32), g_scratch[0], w_scratch[0], g_scratch[1], w_scratch[1]],
        prefetch=1, name="upward",
    )(where, *grads, *weights, raw, q, gain, dcol)

    later = window(later_sums, -1, c)
    held = later[8, 16:24].astype(F32)
    gain_grad = (held + around(held, -8)).reshape(1024)

    def outer(*steps):
        shapes = [(2, 1024, 256)] * 2 if steps == (2,) else [(4, 1024, 256)] * len(steps)
        return call(
            functools.partial(weight_kernel, steps), (1,),
            [anywhere] * 5 + [whole((1024, 768))], [whole(h) for h in shapes],
            [sds(h, BF16) for h in shapes],
            [pltpu.VMEM((len(steps), 4, 768, 256), BF16), pltpu.SemaphoreType.DMA((len(steps), 4))],
            prefetch=1, name=f"outer{steps[0]}",
        )(where, *grads, mixed_t)

    mine = ring_scatter(outer(2), lambda: outer(1, 3, 0), send2)
    pick = lambda r: lax.dynamic_index_in_dim(mine, (first + r) % 4, 0, keepdims=False)
    weight_grad = direct_scatter(pick(2), pick(1), pick(3), pick(0), send1)

    q_grad, k_grad, v_grad = call(
        backward_kernel, (4,),
        [pair] * 4 + [whole((768, HD)), whole((1, 768)), lows, slot, per, slot],
        [pair] * 3, [sds((768, 1024), BF16)] * 3, masks, name="backward",
    )(q, k, v, up, dcol, drow, low, carry, later, later)
    return layer_out, q_grad, k_grad, v_grad, weight_grad, gain_grad


def solution(mesh):
    rows = P(("seq", "ctx"), "tp")
    return jax.shard_map(
        local,
        mesh=mesh,
        in_specs=(rows, rows, rows, P(("seq", "ctx")), P("tp"), P("tp", "ctx"), rows),
        out_specs=(rows, rows, rows, rows, P(("seq", "tp"), "ctx"), P(("seq", "tp"))),
        check_vma=False,
    )
```
